32 devices in a mesh: ep: 16 (over z, x, core), tp: 2 (over y).
Axes of the slice: x: 2, y: 2, z: 4, core: 2. Of those that a mesh axis runs over, the one named last changes fastest.
Arguments:
- tokens: bfloat16 [512, 7168], P('ep', 'tp'), may hold values from -6 to 6
- routes: int32 [512, 8], P('ep'), may hold values from 0 to 15, all different within a row; in each aligned block of 32 rows (0 to 31, 32 to 63, ...) at most 32 rows name the same one
- route_weights: float32 [512, 8], P('ep'), may hold values from 0.05 to 1
- gate_proj: bfloat16 [16, 7168, 1024], P('ep', None, 'tp'), may hold values from -0.0625 to 0.0625
- up_proj: bfloat16 [16, 7168, 1024], P('ep', None, 'tp'), may hold values from -0.0625 to 0.0625
- down_proj: bfloat16 [16, 1024, 7168], P('ep', 'tp'), may hold values from -0.1875 to 0.1875
Outputs:
- mixed: bfloat16 [512, 7168], P('ep', 'tp')
The draws below stay inside these ranges and needn't reach their ends.
Inputs may be any that keep to these rules, and one draw needn't show every extreme that they name: `routes`: each token names 8 different experts; among the 32 tokens of one index of ep no expert is named more than 32 times.
All inputs are finite; a program needn't handle non-finite values.
Results may differ from the reference program's by a relative error of at most 0.012.
Values may be sent and summed in bfloat16 or wider, within the bound.
A program may use at most 64 MiB of HBM per device.

```python
import math
import jax
import jax.numpy as jnp
import numpy as np
from jax import lax

D = 7168
FF = 1024
TOP = 8
TOK_EP = 32
N_EXP = 16
TOKENS = 512
CAP = 32
N_EP = 16
N_TP = 2


def shard_levels(rng, shape, split, low, high):
    level, own = 1.0, jax.random.fold_in(rng, 6)
    for dim, blocks in split:
        draws = jnp.exp(jax.random.uniform(jax.random.fold_in(own, dim), (blocks,), jnp.float32, low / len(split), high / len(split)))
        level = level * jnp.repeat(draws, shape[dim] // blocks).reshape([-1 if axis == dim else 1 for axis in range(len(shape))])
    return level


def deal_out(rng, own, number, rows, amount, top, limit, skew):
    sequence = jax.random.permutation(rng, amount)
    packed, ordinary = load_shares(amount, rows * top, limit, skew, True), load_shares(amount, rows * top, limit, skew, False)
    places = jnp.arange(amount)

    def named(tallies, turn):
        used = int((tallies > 0).sum())
        fixed = max(1, used // 4)
        moved = fixed + (places - fixed + turn * (used - fixed)) % max(1, amount - fixed)
        return jnp.zeros((amount,), jnp.int32).at[sequence[jnp.where(places < fixed, places, moved)]].set(jnp.asarray(tallies, jnp.int32))

    tallies = jnp.where(number % 4 == 0, named(packed, number // 4), named(ordinary, number - number // 4 - 1))
    mixed = jax.random.permutation(jax.random.fold_in(own, 3), amount)
    source_of, sink = mixed[0:amount // 2 * 2:2], mixed[1:amount // 2 * 2:2]
    room = jnp.minimum(tallies[source_of] - 1, limit - tallies[sink]) // 2
    room = jnp.where((source_of == sequence[0]) | (sink == sequence[0]) | (tallies[sink] == 0), 0, jnp.maximum(room, 0))
    moved = jax.random.randint(jax.random.fold_in(own, 4), (amount // 2,), 0, 1 << 20) % (room + 1)
    tallies = tallies.at[source_of].add(-moved).at[sink].add(moved)
    members = jnp.searchsorted(jnp.cumsum(tallies), jnp.arange(rows * top), side="right").astype(jnp.int32)
    listing = members.reshape(top, rows).T
    listing = listing[jax.random.permutation(jax.random.fold_in(own, 1), rows)]
    turn = jax.random.randint(jax.random.fold_in(own, 2), (rows, 1), 0, top)
    return jnp.take_along_axis(listing, (jnp.arange(top)[None, :] + turn) % top, axis=1)


def load_shares(number_of, total, limit, skew, full):
    portions = [(1 << 20) // math.isqrt(grade ** skew) + 1 for grade in range(1, number_of + 1)]
    largest = limit if full else min(limit, max(-(-total // number_of), total * portions[0] // sum(portions)))
    least = 1 if total - largest >= number_of - 1 else 0
    holding, rest = [largest] + [least] * (number_of - 1), total - largest - least * (number_of - 1)
    while rest > 0:
        free = [i for i in range(1, number_of) if holding[i] < largest] or [i for i in range(1, number_of) if holding[i] < limit]
        whole, left = sum([portions[i] for i in free]), rest
        for i in free:
            extra = min(limit - holding[i], max(1, left * portions[i] // whole), rest)
            holding[i] = holding[i] + extra
            rest = rest - extra
    return np.array(holding)


def centred(key, extent, width, bound, split=(), kind=jnp.bfloat16):
    array = jax.random.normal(key, extent, jnp.float32) * width
    if len(split) > 0:
        array = shard_levels(key, extent, split, -0.22, 0.18) * array
    return jnp.clip(array, min=-bound, max=bound).astype(kind)


def setup_inputs(seed: int = 0) -> dict:
    splits = jax.random.split(jax.random.key(seed), 7)
    tokens = centred(splits[0], (TOKENS, D), 1.0, 6.0, ((0, 16), (1, 2)))
    routes_keys = jax.random.split(jax.random.fold_in(splits[1], 1), TOKENS // TOK_EP)
    routes_turns = jax.random.permutation(jax.random.fold_in(splits[1], 3), TOKENS // TOK_EP)
    routes = jax.vmap(lambda own, number: deal_out(jax.random.fold_in(splits[1], 2), own, number, TOK_EP, N_EXP, TOP, CAP, 2))(routes_keys, routes_turns).reshape((TOKENS, TOP))
    route_weights = jnp.clip(jnp.exp(math.log(1.0) - 2.9957323 * jax.random.uniform(splits[2], (TOKENS, TOP), jnp.float32) ** shard_levels(splits[2], (TOKENS, TOP), ((0, 16),), -0.2, 0.2)), 0.05, 1.0)
    gate_proj = centred(splits[3], (N_EXP, D, FF), D ** -0.5, 0.0625, ((0, 16), (2, 2)))
    up_proj = centred(splits[4], (N_EXP, D, FF), D ** -0.5, 0.0625, ((0, 16), (2, 2)))
    down_proj = centred(splits[5], (N_EXP, FF, D), FF ** -0.5, 0.1875, ((0, 16), (1, 2)))
    return dict(tokens=tokens, routes=routes, route_weights=route_weights, gate_proj=gate_proj, up_proj=up_proj, down_proj=down_proj)


def run_expert(inputs):
    expert_rows, w_gate, w_up, w_down = inputs
    gate_act = jnp.dot(expert_rows, w_gate, preferred_element_type=jnp.float32)
    up_act = jnp.dot(expert_rows, w_up, preferred_element_type=jnp.float32)
    hidden = (jax.nn.silu(gate_act) * up_act).astype(jnp.bfloat16)
    part_size = FF // N_TP
    totals = jnp.zeros((expert_rows.shape[0], D), jnp.float32)
    for block_index in range(N_TP):
        low = block_index * part_size
        partial_value = jnp.dot(hidden[:, low:low + part_size], w_down[low:low + part_size], preferred_element_type=jnp.float32)
        totals = totals + lax.optimization_barrier(partial_value.astype(jnp.bfloat16)).astype(jnp.float32)
    return totals.astype(jnp.bfloat16)


def reference(tokens, routes, route_weights, gate_proj, up_proj, down_proj):
    per_block = TOK_EP * TOP
    blocks = routes.reshape(N_EP, per_block).astype(jnp.int32)
    onehot = (blocks[:, :, None] == jnp.arange(N_EXP, dtype=jnp.int32)[None, None, :]).astype(jnp.int32)
    before = jnp.cumsum(onehot, axis=1) - onehot
    position = jnp.sum(before * onehot, axis=2).astype(jnp.int32)
    sources = jnp.arange(N_EP, dtype=jnp.int32)[:, None]
    target = (blocks * (N_EP * CAP) + sources * CAP + position).reshape(-1).astype(jnp.int32)
    owners = jnp.repeat(jnp.arange(TOKENS, dtype=jnp.int32), TOP)
    buffer = jnp.zeros((N_EXP * N_EP * CAP, D), jnp.bfloat16).at[target].set(tokens[owners])
    buffer = buffer.reshape(N_EXP, N_EP * CAP, D)
    results = lax.map(run_expert, (buffer, gate_proj, up_proj, down_proj)).reshape(-1, D)
    picked = results[target].astype(jnp.float32).reshape(TOKENS, TOP, D)
    mixed = jnp.sum(picked * route_weights[:, :, None].astype(jnp.float32), axis=1)
    return mixed.astype(jnp.bfloat16)
```

```python
import jax
import jax.numpy as jnp
from jax import lax
from jax.sharding import PartitionSpec as P


def by_slots(tokens, routes, route_weights, gate_proj, up_proj, down_proj, capacity):
    w_gate = gate_proj[0]
    w_up = up_proj[0]
    w_down = down_proj[0]
    tok_count = tokens.shape[0]
    fanout = routes.shape[1]
    experts = lax.axis_size("ep")
    slot_count = experts * capacity
    flat_ids = routes.reshape(-1)
    onehot = (flat_ids[:, None] == jnp.arange(experts, dtype=jnp.int32)[None, :]).astype(jnp.int32)
    before = jnp.cumsum(onehot, axis=0) - onehot
    position = jnp.sum(before * onehot, axis=1)
    target = flat_ids * capacity + position
    select = jnp.any(
        target.reshape(tok_count, fanout)[None, :, :]
        == jnp.arange(slot_count, dtype=jnp.int32)[:, None, None],
        axis=2,
    ).astype(jnp.bfloat16)
    whole = lax.all_gather(tokens, "tp", axis=1, tiled=True)
    sending = jnp.dot(select, whole, preferred_element_type=jnp.float32).astype(jnp.bfloat16)
    arrived = lax.all_to_all(sending, "ep", split_axis=0, concat_axis=0, tiled=True)
    gate_act = jnp.dot(arrived, w_gate, preferred_element_type=jnp.float32)
    up_act = jnp.dot(arrived, w_up, preferred_element_type=jnp.float32)
    hidden = (jax.nn.silu(gate_act) * up_act).astype(jnp.bfloat16)
    partial_value = jnp.dot(hidden, w_down, preferred_element_type=jnp.float32)
    summed = lax.psum_scatter(
        partial_value.astype(jnp.bfloat16), "tp", scatter_dimension=1, tiled=True
    )
    back_rows = lax.all_to_all(summed, "ep", split_axis=0, concat_axis=0, tiled=True)
    picked = jnp.take(back_rows, target, axis=0).astype(jnp.float32)
    weighted = picked * route_weights.reshape(-1)[:, None]
    mixed = jnp.sum(weighted.reshape(tok_count, fanout, -1), axis=1)
    return mixed.astype(jnp.bfloat16)


def by_tokens(tokens, routes, route_weights, gate_proj, up_proj, down_proj):
    experts = lax.axis_size("ep")
    chosen = routes[:, :, None] == jnp.arange(experts, dtype=jnp.int32)
    dense = jnp.sum(jnp.where(chosen, route_weights[:, :, None], 0.0), axis=1)
    mine = lax.all_to_all(dense.T, "ep", split_axis=0, concat_axis=0, tiled=True).reshape(-1)
    half = lax.all_gather(tokens, "ep", axis=0, tiled=True)
    rows = lax.all_gather(half, "tp", axis=1, tiled=True)
    gate_act = jnp.dot(rows, gate_proj[0], preferred_element_type=jnp.float32)
    up_act = jnp.dot(rows, up_proj[0], preferred_element_type=jnp.float32)
    hidden = (jax.nn.silu(gate_act) * up_act * mine[:, None]).astype(jnp.bfloat16)
    partial_value = jnp.dot(hidden, down_proj[0], preferred_element_type=jnp.float32)
    summed = lax.psum_scatter(
        partial_value.astype(jnp.bfloat16), "tp", scatter_dimension=1, tiled=True
    )
    return lax.psum_scatter(summed, "ep", scatter_dimension=0, tiled=True)


def per_device(tokens, routes, *rest):
    tok_count = tokens.shape[0]
    capacity = min(tok_count, max(2, 2 * tok_count * routes.shape[1] // lax.axis_size("ep")))
    if capacity == tok_count:
        return by_tokens(tokens, routes, *rest)
    return by_slots(tokens, routes, *rest, capacity)


def solution(mesh):
    in_specs = (
        P("ep", "tp"),
        P("ep", None),
        P("ep", None),
        P("ep", None, "tp"),
        P("ep", None, "tp"),
        P("ep", "tp", None),
    )
    out_specs = P("ep", "tp")
    return jax.shard_map(
        per_device, mesh=mesh, in_specs=in_specs, out_specs=out_specs, check_vma=False
    )
```

```python
import functools
import heapq
import itertools

import jax
import jax.numpy as jnp
from jax import lax
from jax.experimental import pallas as pl
from jax.experimental.pallas import tpu as pltpu
from jax.sharding import PartitionSpec as P


def by_slots(tokens, routes, route_weights, gate_proj, up_proj, down_proj, capacity):
    w_gate = gate_proj[0]
    w_up = up_proj[0]
    w_down = down_proj[0]
    tok_count = tokens.shape[0]
    fanout = routes.shape[1]
    experts = lax.axis_size("ep")
    slot_count = experts * capacity
    flat_ids = routes.reshape(-1)
    onehot = (flat_ids[:, None] == jnp.arange(experts, dtype=jnp.int32)[None, :]).astype(jnp.int32)
    before = jnp.cumsum(onehot, axis=0) - onehot
    position = jnp.sum(before * onehot, axis=1)
    target = flat_ids * capacity + position
    select = jnp.any(
        target.reshape(tok_count, fanout)[None, :, :]
        == jnp.arange(slot_count, dtype=jnp.int32)[:, None, None],
        axis=2,
    ).astype(jnp.bfloat16)
    whole = lax.all_gather(tokens, "tp", axis=1, tiled=True)
    sending = jnp.dot(select, whole, preferred_element_type=jnp.float32).astype(jnp.bfloat16)
    arrived = lax.all_to_all(sending, "ep", split_axis=0, concat_axis=0, tiled=True)
    gate_act = jnp.dot(arrived, w_gate, preferred_element_type=jnp.float32)
    up_act = jnp.dot(arrived, w_up, preferred_element_type=jnp.float32)
    hidden = (jax.nn.silu(gate_act) * up_act).astype(jnp.bfloat16)
    partial_value = jnp.dot(hidden, w_down, preferred_element_type=jnp.float32)
    summed = lax.psum_scatter(
        partial_value.astype(jnp.bfloat16), "tp", scatter_dimension=1, tiled=True
    )
    back_rows = lax.all_to_all(summed, "ep", split_axis=0, concat_axis=0, tiled=True)
    picked = jnp.take(back_rows, target, axis=0).astype(jnp.float32)
    weighted = picked * route_weights.reshape(-1)[:, None]
    mixed = jnp.sum(weighted.reshape(tok_count, fanout, -1), axis=1)
    return mixed.astype(jnp.bfloat16)


LINK = 46e3
PAIR = 150e3


def edges(order, block, ring):
    place = dict(zip("zxy", block))
    stage = max([i for i, axis in enumerate(order) if place[axis]], default=-1)
    out = []
    for i in range(max(stage, 0), len(order)):
        axis = order[i]
        limit = ring - 1 if axis == "z" else 1
        if place[axis] < limit:
            out.append((axis, tuple(place[a] + (a == axis) for a in "zxy")))
    return out


def make_plan(parts, ring, rows, gate_us, down_us):
    heap, ops, count, free = [], [], itertools.count(), {}
    clock = 0.0

    def push(time, *event):
        heapq.heappush(heap, (time, next(count), event))

    def send(link, size, rate, delay):
        free[link] = max(clock, free.get(link, 0.0)) + size / rate
        return free[link] + delay

    held, finished, made, got = {}, {}, {}, {}
    blocks = [(z, x, y) for z in range(ring) for x in range(2) for y in range(2)]
    children = {(p, b): [c for _, c in edges(order, b, ring)] for p, (order, _, _) in enumerate(parts) for b in blocks}
    parent = {(p, c): b for (p, b), cs in children.items() for c in cs}

    def hold(block):
        key = (block[0], block[2])
        held[key] = held.get(key, 0) + 1
        if held[key] == 4 * len(parts):
            push(clock, "gate", *key)

    def reach(p, block):
        got[p, block] = got.get((p, block), 0) + 1
        if got[p, block] == 1 + len(children[p, block]):
            push(clock, "sum", p, block)

    for p in range(len(parts)):
        push(0.0, "have", p, (0, 0, 0))
    while heap:
        time, _, event = heapq.heappop(heap)
        clock = max(clock, time)
        ops.append(event)
        kind = event[0]
        if kind == "have":
            _, p, block = event
            order, _, width = parts[p]
            for axis, child in edges(order, block, ring):
                push(send(axis, rows * width * 2, LINK, 1.6), "have", p, child)
            push(send("core", rows * width * 2, PAIR, 0.9), "mate", p, block)
            hold(block)
        elif kind == "mate":
            hold(event[2])
        elif kind == "gate":
            clock += gate_us
            finished[event[1]] = finished.get(event[1], 0) + 1
            if finished[event[1]] == 2:
                for y in (1, 0):
                    push(clock, "down", event[1], y)
        elif kind == "down":
            clock += down_us
            width = sum(part[2] for part in parts)
            for x in (1, 0):
                push(send("core", rows * width * 2, PAIR, 0.9), "back", (event[1], x, event[2]))
        elif kind == "back":
            for p in range(len(parts)):
                reach(p, event[1])
        elif kind == "sum":
            _, p, block = event
            clock += 0.1
            if (p, block) in parent:
                axis = [a for a, i, j in zip("zxy", block, parent[p, block]) if i != j][0]
                push(send(axis, rows * parts[p][2] * 2, LINK, 1.6), "came", p, block)
        elif kind == "came":
            reach(event[1], parent[event[1], event[2]])
    return ops, children, parent


def layer_kernel(parts, ring, plan, tokens, shares, gate_hbm, up_hbm, down_hbm, out, everything, w_gate, w_up, w_down,
                 gate_acc, up_acc, hidden, result, mate_rows, landed, weights, own_sem, load_sem, have_send, have_recv,
                 mate_send, mate_recv, back_send, back_recv, sum_send, sum_recv, share_send, share_recv):
    ops, children, parent = plan
    ep, tp = lax.axis_index("ep"), lax.axis_index("tp")
    core, side, level = lax.rem(ep, 2), lax.rem(ep // 2, 2), ep // 4
    rows, half = tokens.shape
    group = 4 * rows

    def device(z=0, x=0, y=0, c=0):
        new_z = lax.rem(level + z + ring, ring)
        new_x = lax.rem(side + x, 2)
        return (new_z * 2 + new_x) * 2 + lax.rem(core + c, 2), lax.rem(tp + y, 2)

    def number(block):
        return (block[0] * 2 + block[1]) * 2 + block[2]

    def place(block, c=0):
        return pl.ds(((block[0] * 2 + block[1]) * 2 + c) * rows, rows)

    def pair_place(block):
        return pl.ds((block[0] * 2 + block[1]) * rows, rows)

    def columns(p):
        return pl.ds(parts[p][1], parts[p][2])

    def remote(src, dst, send, recv, target):
        return pltpu.make_async_remote_copy(src_ref=src, dst_ref=dst, send_sem=send, recv_sem=recv,
                                            device_id=target, device_id_type=pl.DeviceIdType.MESH)

    def have_copy(p, child, axis):
        block = tuple(v - (a == axis) for a, v in zip("zxy", child))
        if block == (0, 0, 0):
            src = tokens.at[:, columns(p)]
        else:
            src = everything.at[block[2], place(block), columns(p)]
        return remote(src, everything.at[child[2], place(child), columns(p)], have_send.at[p, number(child)],
                      have_recv.at[p, number(child)], device(**{axis: 1}))

    def mate_copy(p, block):
        if block == (0, 0, 0):
            src = tokens.at[:, columns(p)]
        else:
            src = everything.at[block[2], place(block), columns(p)]
        return remote(src, everything.at[block[2], place(block, 1), columns(p)], mate_send.at[p, number(block)],
                      mate_recv.at[p, number(block)], device(c=1))

    def back_copy(block):
        return remote(result.at[block[2], place(block, 1)], mate_rows.at[block[2], pair_place(block)],
                      back_send.at[number(block)], back_recv.at[number(block)], device(c=1))

    def sum_copy(p, block):
        axis = [a for a, i, j in zip("zxy", block, parent[p, block]) if i != j][0]
        return remote(result.at[block[2], place(block), columns(p)], landed.at[block[2], pair_place(block), columns(p)],
                      sum_send.at[p, number(block)], sum_recv.at[p, number(block)], device(**{axis: -1 if axis == "z" else 1}))

    peers = [(z, x, c) for z in range(ring) for x in range(2) for c in range(2) if (z, x, c) != (0, 0, 0)]

    def share_copy(peer):
        z, x, c = peer
        target = device(z=z, x=x, c=c)
        i = number(peer)
        return remote(shares.at[target[0]], weights.at[i], share_send.at[i], share_recv.at[i], target)

    loads = []
    for y in range(2):
        at = lax.rem(tp + y, 2) * half
        loads.append([
            pltpu.make_async_copy(gate_hbm.at[pl.ds(at, half)], w_gate.at[y], load_sem.at[y, 0]),
            pltpu.make_async_copy(up_hbm.at[pl.ds(at, half)], w_up.at[y], load_sem.at[y, 1]),
            pltpu.make_async_copy(down_hbm.at[:, pl.ds(pl.multiple_of(at, 128), half)], w_down.at[y], load_sem.at[y, 2]),
        ])
    own = pltpu.make_async_copy(tokens, everything.at[0, pl.ds(0, rows)], own_sem)
    own_share = pltpu.make_async_copy(shares.at[ep], weights.at[0], share_send.at[0])

    own.start()
    own_share.start()
    for kind in ((0, 1), (2,)):
        for y in range(2):
            for i in kind:
                loads[y][i].start()
    barrier = pltpu.get_barrier_semaphore()
    greeted = [device(z=z, x=x, c=c) for z, x, c in peers] + [device(y=1)]
    for target in greeted:
        pl.semaphore_signal(barrier, inc=1, device_id=target, device_id_type=pl.DeviceIdType.MESH)
    pl.semaphore_wait(barrier, len(greeted))
    for peer in peers:
        share_copy(peer).start()

    waited = set()

    def once(key, copy):
        if key not in waited:
            waited.add(key)
            copy.wait()

    def gate(z, y, first, last):
        once("own", own)
        once(("load", y, 0), loads[y][0])
        once(("load", y, 1), loads[y][1])
        here = pl.ds(z * group, group)
        tile = 512 if half % 512 == 0 else 128
        if first:
            gate_acc[here] = jnp.zeros((group, gate_acc.shape[1]), jnp.float32)
            up_acc[here] = jnp.zeros((group, gate_acc.shape[1]), jnp.float32)

        def step(k, carry):
            depth = pl.ds(pl.multiple_of(k * tile, tile), tile)
            x = everything[y, here, depth]
            gate_acc[here] += jnp.dot(x, w_gate[y, depth], preferred_element_type=jnp.float32)
            up_acc[here] += jnp.dot(x, w_up[y, depth], preferred_element_type=jnp.float32)
            return carry

        lax.fori_loop(0, half // tile, step, 0)
        if last:
            for x in range(2):
                for c in range(2):
                    i = number((z, x, c))
                    if i:
                        share_copy((z, x, c)).wait_recv()
                    else:
                        own_share.wait()
                    row = lax.broadcasted_iota(jnp.int32, (rows, 128), 0)
                    lane = lax.broadcasted_iota(jnp.int32, (rows, 128), 1)
                    spread = jnp.broadcast_to(weights[i, 0:1, :], (rows, 128))
                    weight = jnp.sum(jnp.where(row == lane, spread, 0.0), axis=1, keepdims=True)
                    at = pl.ds(i * rows, rows)
                    g = gate_acc[at]
                    hidden[at] = (g / (1.0 + jnp.exp(-g)) * up_acc[at] * weight).astype(hidden.dtype)

    def down(z, y):
        once(("load", y, 2), loads[y][2])
        here = pl.ds(z * group, group)
        tile = 512 if half % 512 == 0 else 128

        def step(k, carry):
            across = pl.ds(pl.multiple_of(k * tile, tile), tile)
            result[y, here, across] = jnp.dot(
                hidden[here], w_down[y, :, across], preferred_element_type=jnp.float32).astype(result.dtype)
            return carry

        lax.fori_loop(0, half // tile, step, 0)

    gates, sent = {}, []
    for event in ops:
        kind = event[0]
        if kind == "have":
            _, p, block = event
            if block != (0, 0, 0):
                axis = [a for a, i, j in zip("zxy", block, parent[p, block]) if i != j][0]
                have_copy(p, block, axis).wait_recv()
            for axis, child in edges(parts[p][0], block, ring):
                have_copy(p, child, axis).start()
                sent.append(have_copy(p, child, axis))
            mate_copy(p, block).start()
            sent.append(mate_copy(p, block))
        elif kind == "mate":
            mate_copy(event[1], event[2]).wait_recv()
        elif kind == "gate":
            z, y = event[1:]
            gates[z] = gates.get(z, 0) + 1
            gate(z, y, gates[z] == 1, gates[z] == 2)
        elif kind == "down":
            z, y = event[1:]
            down(z, y)
            for x in (1, 0):
                back_copy((z, x, y)).start()
                sent.append(back_copy((z, x, y)))
        elif kind == "back":
            back_copy(event[1]).wait_recv()
        elif kind == "came":
            sum_copy(event[1], event[2]).wait_recv()
        elif kind == "sum":
            _, p, block = event
            y = block[2]
            total = result[y, place(block), columns(p)].astype(jnp.float32)
            total += mate_rows[y, pair_place(block), columns(p)].astype(jnp.float32)
            for child in children[p, block]:
                total += landed[child[2], pair_place(child), columns(p)].astype(jnp.float32)
            if (p, block) in parent:
                result[y, place(block), columns(p)] = total.astype(result.dtype)
                sum_copy(p, block).start()
                sent.append(sum_copy(p, block))
            else:
                out[:, columns(p)] = total.astype(out.dtype)
    for copy in sent:
        copy.wait_send()
    for peer in peers:
        share_copy(peer).wait_send()


def by_tokens(tokens, routes, route_weights, gate_proj, up_proj, down_proj):
    experts = lax.axis_size("ep")
    rows, half = tokens.shape
    depth = gate_proj.shape[2]
    ring = experts // 4
    chosen = routes[:, :, None] == jnp.arange(experts, dtype=jnp.int32)
    dense = jnp.sum(jnp.where(chosen, route_weights[:, :, None], 0.0), axis=1)
    shares = jnp.pad(dense.T, ((0, 0), (0, 128 - rows)))
    shares = jnp.broadcast_to(shares[:, None, :], (experts, 8, 128))
    tiles = half // 128
    most = max(1, tiles * 11 // 28)
    widths = [tiles - 2 * most, most, most]
    parts, at = [], 0
    for order, width in zip(("xyz", "zxy", "zyx"), widths):
        parts.append((order, at * 128, width * 128))
        at += width
    plan = make_plan(parts, ring, rows, 1.6, 0.7)
    count, total = 4 * ring, experts * rows
    any_space = pl.BlockSpec(memory_space=pl.ANY)
    vmem = pl.BlockSpec(memory_space=pltpu.VMEM)
    dma = pltpu.SemaphoreType.DMA
    bf16, f32 = jnp.bfloat16, jnp.float32
    return pl.pallas_call(
        functools.partial(layer_kernel, parts, ring, plan),
        out_shape=jax.ShapeDtypeStruct(tokens.shape, tokens.dtype),
        in_specs=[vmem, vmem, any_space, any_space, any_space],
        out_specs=vmem,
        scratch_shapes=[
            pltpu.VMEM((2, total, half), bf16),
            pltpu.VMEM((2, half, depth), bf16),
            pltpu.VMEM((2, half, depth), bf16),
            pltpu.VMEM((2, depth, half), bf16),
            pltpu.VMEM((total, depth), f32),
            pltpu.VMEM((total, depth), f32),
            pltpu.VMEM((total, depth), bf16),
            pltpu.VMEM((2, total, half), bf16),
            pltpu.VMEM((2, total // 2, half), bf16),
            pltpu.VMEM((2, total // 2, half), bf16),
            pltpu.VMEM((experts, 8, 128), f32),
            dma, dma((2, 3)),
            dma((3, count)), dma((3, count)),
            dma((3, count)), dma((3, count)),
            dma((count,)), dma((count,)),
            dma((3, count)), dma((3, count)),
            dma((experts,)), dma((experts,)),
        ],
        compiler_params=pltpu.CompilerParams(
            collective_id=0, has_side_effects=True, vmem_limit_bytes=60 << 20),
    )(tokens, shares, gate_proj[0], up_proj[0], down_proj[0])


def per_device(tokens, routes, *rest):
    tok_count = tokens.shape[0]
    capacity = min(tok_count, max(2, 2 * tok_count * routes.shape[1] // lax.axis_size("ep")))
    if capacity == tok_count and tok_count % 16 == 0 and tok_count <= 128 and lax.axis_size("ep") % 4 == 0 and lax.axis_size("tp") == 2:
        return by_tokens(tokens, routes, *rest)
    return by_slots(tokens, routes, *rest, capacity)


def solution(mesh):
    in_specs = (
        P("ep", "tp"),
        P("ep", None),
        P("ep", None),
        P("ep", None, "tp"),
        P("ep", None, "tp"),
        P("ep", "tp", None),
    )
    out_specs = P("ep", "tp")
    return jax.shard_map(
        per_device, mesh=mesh, in_specs=in_specs, out_specs=out_specs, check_vma=False
    )
```

```python
import functools
import heapq
import itertools

import jax
import jax.numpy as jnp
from jax import lax
from jax.experimental import pallas as pl
from jax.experimental.pallas import tpu as pltpu
from jax.sharding import PartitionSpec as P


def by_slots(tokens, routes, route_weights, gate_proj, up_proj, down_proj, capacity):
    w_gate = gate_proj[0]
    w_up = up_proj[0]
    w_down = down_proj[0]
    tok_count = tokens.shape[0]
    fanout = routes.shape[1]
    experts = lax.axis_size("ep")
    slot_count = experts * capacity
    flat_ids = routes.reshape(-1)
    onehot = (flat_ids[:, None] == jnp.arange(experts, dtype=jnp.int32)[None, :]).astype(jnp.int32)
    before = jnp.cumsum(onehot, axis=0) - onehot
    position = jnp.sum(before * onehot, axis=1)
    target = flat_ids * capacity + position
    select = jnp.any(
        target.reshape(tok_count, fanout)[None, :, :]
        == jnp.arange(slot_count, dtype=jnp.int32)[:, None, None],
        axis=2,
    ).astype(jnp.bfloat16)
    whole = lax.all_gather(tokens, "tp", axis=1, tiled=True)
    sending = jnp.dot(select, whole, preferred_element_type=jnp.float32).astype(jnp.bfloat16)
    arrived = lax.all_to_all(sending, "ep", split_axis=0, concat_axis=0, tiled=True)
    gate_act = jnp.dot(arrived, w_gate, preferred_element_type=jnp.float32)
    up_act = jnp.dot(arrived, w_up, preferred_element_type=jnp.float32)
    hidden = (jax.nn.silu(gate_act) * up_act).astype(jnp.bfloat16)
    partial_value = jnp.dot(hidden, w_down, preferred_element_type=jnp.float32)
    summed = lax.psum_scatter(
        partial_value.astype(jnp.bfloat16), "tp", scatter_dimension=1, tiled=True
    )
    back_rows = lax.all_to_all(summed, "ep", split_axis=0, concat_axis=0, tiled=True)
    picked = jnp.take(back_rows, target, axis=0).astype(jnp.float32)
    weighted = picked * route_weights.reshape(-1)[:, None]
    mixed = jnp.sum(weighted.reshape(tok_count, fanout, -1), axis=1)
    return mixed.astype(jnp.bfloat16)


LINK = 40e3
PAIR = 300e3


def edges(order, block, ring):
    place = dict(zip("zxy", block))
    stage = max([i for i, axis in enumerate(order) if place[axis]], default=-1)
    out = []
    for i in range(max(stage, 0), len(order)):
        axis = order[i]
        limit = ring - 1 if axis == "z" else 1
        if place[axis] < limit:
            out.append((axis, tuple(place[a] + (a == axis) for a in "zxy")))
    return out


def make_plan(parts, ring, rows, gate_us, down_us):
    heap, ops, count, free = [], [], itertools.count(), {}
    clock = 0.0

    def push(time, *event):
        heapq.heappush(heap, (time, next(count), event))

    def send(link, size, rate, delay):
        free[link] = max(clock, free.get(link, 0.0)) + size / rate
        return free[link] + delay

    held, finished, made, got = {}, {}, {}, {}
    blocks = [(z, x, y) for z in range(ring) for x in range(2) for y in range(2)]
    children = {(p, b): [c for _, c in edges(order, b, ring)] for p, (order, _, _) in enumerate(parts) for b in blocks}
    parent = {(p, c): b for (p, b), cs in children.items() for c in cs}

    def hold(block):
        key = (block[0], block[2])
        held[key] = held.get(key, 0) + 1
        if held[key] == 4 * len(parts):
            push(clock, "gate", *key)

    def reach(p, block):
        got[p, block] = got.get((p, block), 0) + 1
        if got[p, block] == 1 + len(children[p, block]):
            push(clock, "sum", p, block)

    for p in range(len(parts)):
        push(0.0, "have", p, (0, 0, 0))
    while heap:
        time, _, event = heapq.heappop(heap)
        clock = max(clock, time)
        ops.append(event)
        kind = event[0]
        if kind == "have":
            _, p, block = event
            order, _, width = parts[p]
            for axis, child in edges(order, block, ring):
                push(send(axis, rows * width * 2, LINK, 1.6), "have", p, child)
            push(send("core", rows * width * 2, PAIR, 0.9), "mate", p, block)
            hold(block)
        elif kind == "mate":
            hold(event[2])
        elif kind == "gate":
            clock += gate_us
            finished[event[1]] = finished.get(event[1], 0) + 1
            if finished[event[1]] == 2:
                for y in (1, 0):
                    push(clock, "down", event[1], y)
        elif kind == "down":
            clock += down_us
            width = sum(part[2] for part in parts)
            for x in (1, 0):
                push(send("core", rows * width * 2, PAIR, 0.9), "back", (event[1], x, event[2]))
        elif kind == "back":
            for p in range(len(parts)):
                reach(p, event[1])
        elif kind == "sum":
            _, p, block = event
            clock += 0.1
            if (p, block) in parent:
                axis = [a for a, i, j in zip("zxy", block, parent[p, block]) if i != j][0]
                push(send(axis, rows * parts[p][2] * 2, LINK, 1.6), "came", p, block)
        elif kind == "came":
            reach(event[1], parent[event[1], event[2]])
    return ops, children, parent


def layer_kernel(parts, ring, plan, tokens, shares, gate_hbm, up_hbm, down_hbm, out, everything, w_gate, w_up, w_down,
                 gate_acc, up_acc, hidden, result, mate_rows, landed, weights, own_sem, load_sem, have_send, have_recv,
                 mate_send, mate_recv, back_send, back_recv, sum_send, sum_recv, share_send, share_recv):
    ops, children, parent = plan
    ep, tp = lax.axis_index("ep"), lax.axis_index("tp")
    core, side, level = lax.rem(ep, 2), lax.rem(ep // 2, 2), ep // 4
    rows, half = tokens.shape
    group = 4 * rows

    def device(z=0, x=0, y=0, c=0):
        new_z = lax.rem(level + z + ring, ring)
        new_x = lax.rem(side + x, 2)
        return (new_z * 2 + new_x) * 2 + lax.rem(core + c, 2), lax.rem(tp + y, 2)

    def number(block):
        return (block[0] * 2 + block[1]) * 2 + block[2]

    def place(block, c=0):
        return pl.ds(((block[0] * 2 + block[1]) * 2 + c) * rows, rows)

    def pair_place(block):
        return pl.ds((block[0] * 2 + block[1]) * rows, rows)

    def columns(p):
        return pl.ds(parts[p][1], parts[p][2])

    def remote(src, dst, send, recv, target):
        return pltpu.make_async_remote_copy(src_ref=src, dst_ref=dst, send_sem=send, recv_sem=recv,
                                            device_id=target, device_id_type=pl.DeviceIdType.MESH)

    def have_copy(p, child, axis):
        block = tuple(v - (a == axis) for a, v in zip("zxy", child))
        if block == (0, 0, 0):
            src = tokens.at[:, columns(p)]
        else:
            src = everything.at[block[2], place(block), columns(p)]
        return remote(src, everything.at[child[2], place(child), columns(p)], have_send.at[p, number(child)],
                      have_recv.at[p, number(child)], device(**{axis: 1}))

    def mate_copy(p, block):
        if block == (0, 0, 0):
            src = tokens.at[:, columns(p)]
        else:
            src = everything.at[block[2], place(block), columns(p)]
        return remote(src, everything.at[block[2], place(block, 1), columns(p)], mate_send.at[p, number(block)],
                      mate_recv.at[p, number(block)], device(c=1))

    def back_copy(block):
        return remote(result.at[block[2], place(block, 1)], mate_rows.at[block[2], pair_place(block)],
                      back_send.at[number(block)], back_recv.at[number(block)], device(c=1))

    def sum_copy(p, block):
        axis = [a for a, i, j in zip("zxy", block, parent[p, block]) if i != j][0]
        return remote(result.at[block[2], place(block), columns(p)], landed.at[block[2], pair_place(block), columns(p)],
                      sum_send.at[p, number(block)], sum_recv.at[p, number(block)], device(**{axis: -1 if axis == "z" else 1}))

    peers = [(z, x, c) for z in range(ring) for x in range(2) for c in range(2) if (z, x, c) != (0, 0, 0)]

    def share_copy(peer):
        z, x, c = peer
        target = device(z=z, x=x, c=c)
        i = number(peer)
        return remote(shares.at[target[0]], weights.at[i], share_send.at[i], share_recv.at[i], target)

    loads = []
    for y in range(2):
        at = lax.rem(tp + y, 2) * half
        loads.append([
            pltpu.make_async_copy(gate_hbm.at[pl.ds(at, half)], w_gate.at[y], load_sem.at[y, 0]),
            pltpu.make_async_copy(up_hbm.at[pl.ds(at, half)], w_up.at[y], load_sem.at[y, 1]),
            pltpu.make_async_copy(down_hbm.at[:, pl.ds(pl.multiple_of(at, 128), half)], w_down.at[y], load_sem.at[y, 2]),
        ])
    own = pltpu.make_async_copy(tokens, everything.at[0, pl.ds(0, rows)], own_sem)
    own_share = pltpu.make_async_copy(shares.at[ep], weights.at[0], share_send.at[0])

    own.start()
    own_share.start()
    for kind in ((0, 1), (2,)):
        for y in range(2):
            for i in kind:
                loads[y][i].start()
    barrier = pltpu.get_barrier_semaphore()
    greeted = [device(z=z, x=x, c=c) for z, x, c in peers] + [device(y=1)]
    for target in greeted:
        pl.semaphore_signal(barrier, inc=1, device_id=target, device_id_type=pl.DeviceIdType.MESH)
    pl.semaphore_wait(barrier, len(greeted))
    for peer in peers:
        share_copy(peer).start()

    waited = set()

    def once(key, copy):
        if key not in waited:
            waited.add(key)
            copy.wait()

    def gate(z, y, first, last):
        once("own", own)
        once(("load", y, 0), loads[y][0])
        once(("load", y, 1), loads[y][1])
        here = pl.ds(z * group, group)
        tile = 512 if half % 512 == 0 else 128
        if first:
            gate_acc[here] = jnp.zeros((group, gate_acc.shape[1]), jnp.float32)
            up_acc[here] = jnp.zeros((group, gate_acc.shape[1]), jnp.float32)

        def step(k, carry):
            depth = pl.ds(pl.multiple_of(k * tile, tile), tile)
            x = everything[y, here, depth]
            gate_acc[here] += jnp.dot(x, w_gate[y, depth], preferred_element_type=jnp.float32)
            up_acc[here] += jnp.dot(x, w_up[y, depth], preferred_element_type=jnp.float32)
            return carry

        lax.fori_loop(0, half // tile, step, 0)
        if last:
            for x in range(2):
                for c in range(2):
                    i = number((z, x, c))
                    if i:
                        share_copy((z, x, c)).wait_recv()
                    else:
                        own_share.wait()
                    row = lax.broadcasted_iota(jnp.int32, (rows, 128), 0)
                    lane = lax.broadcasted_iota(jnp.int32, (rows, 128), 1)
                    spread = jnp.broadcast_to(weights[i, 0:1, :], (rows, 128))
                    weight = jnp.sum(jnp.where(row == lane, spread, 0.0), axis=1, keepdims=True)
                    at = pl.ds(i * rows, rows)
                    g = gate_acc[at]
                    hidden[at] = (g / (1.0 + jnp.exp(-g)) * up_acc[at] * weight).astype(hidden.dtype)

    def down(z, y):
        once(("load", y, 2), loads[y][2])
        here = pl.ds(z * group, group)
        tile = 512 if half % 512 == 0 else 128

        def step(k, carry):
            across = pl.ds(pl.multiple_of(k * tile, tile), tile)
            result[y, here, across] = jnp.dot(
                hidden[here], w_down[y, :, across], preferred_element_type=jnp.float32).astype(result.dtype)
            return carry

        lax.fori_loop(0, half // tile, step, 0)

    gates, sent = {}, []
    for event in ops:
        kind = event[0]
        if kind == "have":
            _, p, block = event
            if block != (0, 0, 0):
                axis = [a for a, i, j in zip("zxy", block, parent[p, block]) if i != j][0]
                have_copy(p, block, axis).wait_recv()
            for axis, child in edges(parts[p][0], block, ring):
                have_copy(p, child, axis).start()
                sent.append(have_copy(p, child, axis))
            mate_copy(p, block).start()
            sent.append(mate_copy(p, block))
        elif kind == "mate":
            mate_copy(event[1], event[2]).wait_recv()
        elif kind == "gate":
            z, y = event[1:]
            gates[z] = gates.get(z, 0) + 1
            gate(z, y, gates[z] == 1, gates[z] == 2)
        elif kind == "down":
            z, y = event[1:]
            down(z, y)
            for x in (1, 0):
                back_copy((z, x, y)).start()
                sent.append(back_copy((z, x, y)))
        elif kind == "back":
            back_copy(event[1]).wait_recv()
        elif kind == "came":
            sum_copy(event[1], event[2]).wait_recv()
        elif kind == "sum":
            _, p, block = event
            y = block[2]
            total = result[y, place(block), columns(p)].astype(jnp.float32)
            total += mate_rows[y, pair_place(block), columns(p)].astype(jnp.float32)
            for child in children[p, block]:
                total += landed[child[2], pair_place(child), columns(p)].astype(jnp.float32)
            if (p, block) in parent:
                result[y, place(block), columns(p)] = total.astype(result.dtype)
                sum_copy(p, block).start()
                sent.append(sum_copy(p, block))
            else:
                out[:, columns(p)] = total.astype(out.dtype)
    for copy in sent:
        copy.wait_send()
    for peer in peers:
        share_copy(peer).wait_send()


def by_tokens(tokens, routes, route_weights, gate_proj, up_proj, down_proj):
    experts = lax.axis_size("ep")
    rows, half = tokens.shape
    depth = gate_proj.shape[2]
    ring = experts // 4
    chosen = routes[:, :, None] == jnp.arange(experts, dtype=jnp.int32)
    dense = jnp.sum(jnp.where(chosen, route_weights[:, :, None], 0.0), axis=1)
    shares = jnp.pad(dense.T, ((0, 0), (0, 128 - rows)))
    shares = jnp.broadcast_to(shares[:, None, :], (experts, 8, 128))
    tiles = half // 128
    most = max(1, tiles * 11 // 28)
    widths = [tiles - 2 * most, most, most]
    parts, at = [], 0
    for order, width in zip(("xyz", "zxy", "zyx"), widths):
        parts.append((order, at * 128, width * 128))
        at += width
    plan = make_plan(parts, ring, rows, 2.0, 1.6)
    count, total = 4 * ring, experts * rows
    any_space = pl.BlockSpec(memory_space=pl.ANY)
    vmem = pl.BlockSpec(memory_space=pltpu.VMEM)
    dma = pltpu.SemaphoreType.DMA
    bf16, f32 = jnp.bfloat16, jnp.float32
    return pl.pallas_call(
        functools.partial(layer_kernel, parts, ring, plan),
        out_shape=jax.ShapeDtypeStruct(tokens.shape, tokens.dtype),
        in_specs=[vmem, vmem, any_space, any_space, any_space],
        out_specs=vmem,
        scratch_shapes=[
            pltpu.VMEM((2, total, half), bf16),
            pltpu.VMEM((2, half, depth), bf16),
            pltpu.VMEM((2, half, depth), bf16),
            pltpu.VMEM((2, depth, half), bf16),
            pltpu.VMEM((total, depth), f32),
            pltpu.VMEM((total, depth), f32),
            pltpu.VMEM((total, depth), bf16),
            pltpu.VMEM((2, total, half), bf16),
            pltpu.VMEM((2, total // 2, half), bf16),
            pltpu.VMEM((2, total // 2, half), bf16),
            pltpu.VMEM((experts, 8, 128), f32),
            dma, dma((2, 3)),
            dma((3, count)), dma((3, count)),
            dma((3, count)), dma((3, count)),
            dma((count,)), dma((count,)),
            dma((3, count)), dma((3, count)),
            dma((experts,)), dma((experts,)),
        ],
        compiler_params=pltpu.CompilerParams(
            collective_id=0, has_side_effects=True, vmem_limit_bytes=60 << 20),
    )(tokens, shares, gate_proj[0], up_proj[0], down_proj[0])


def per_device(tokens, routes, *rest):
    tok_count = tokens.shape[0]
    capacity = min(tok_count, max(2, 2 * tok_count * routes.shape[1] // lax.axis_size("ep")))
    if capacity == tok_count and tok_count % 16 == 0 and tok_count <= 128 and lax.axis_size("ep") % 4 == 0 and lax.axis_size("tp") == 2:
        return by_tokens(tokens, routes, *rest)
    return by_slots(tokens, routes, *rest, capacity)


def solution(mesh):
    in_specs = (
        P("ep", "tp"),
        P("ep", None),
        P("ep", None),
        P("ep", None, "tp"),
        P("ep", None, "tp"),
        P("ep", "tp", None),
    )
    out_specs = P("ep", "tp")
    return jax.shard_map(
        per_device, mesh=mesh, in_specs=in_specs, out_specs=out_specs, check_vma=False
    )
```

```python
import functools
import heapq
import itertools

import jax
import jax.numpy as jnp
from jax import lax
from jax.experimental import pallas as pl
from jax.experimental.pallas import tpu as pltpu
from jax.sharding import PartitionSpec as P


def by_slots(tokens, routes, route_weights, gate_proj, up_proj, down_proj, capacity):
    w_gate = gate_proj[0]
    w_up = up_proj[0]
    w_down = down_proj[0]
    tok_count = tokens.shape[0]
    fanout = routes.shape[1]
    experts = lax.axis_size("ep")
    slot_count = experts * capacity
    flat_ids = routes.reshape(-1)
    onehot = (flat_ids[:, None] == jnp.arange(experts, dtype=jnp.int32)[None, :]).astype(jnp.int32)
    before = jnp.cumsum(onehot, axis=0) - onehot
    position = jnp.sum(before * onehot, axis=1)
    target = flat_ids * capacity + position
    select = jnp.any(
        target.reshape(tok_count, fanout)[None, :, :]
        == jnp.arange(slot_count, dtype=jnp.int32)[:, None, None],
        axis=2,
    ).astype(jnp.bfloat16)
    whole = lax.all_gather(tokens, "tp", axis=1, tiled=True)
    sending = jnp.dot(select, whole, preferred_element_type=jnp.float32).astype(jnp.bfloat16)
    arrived = lax.all_to_all(sending, "ep", split_axis=0, concat_axis=0, tiled=True)
    gate_act = jnp.dot(arrived, w_gate, preferred_element_type=jnp.float32)
    up_act = jnp.dot(arrived, w_up, preferred_element_type=jnp.float32)
    hidden = (jax.nn.silu(gate_act) * up_act).astype(jnp.bfloat16)
    partial_value = jnp.dot(hidden, w_down, preferred_element_type=jnp.float32)
    summed = lax.psum_scatter(
        partial_value.astype(jnp.bfloat16), "tp", scatter_dimension=1, tiled=True
    )
    back_rows = lax.all_to_all(summed, "ep", split_axis=0, concat_axis=0, tiled=True)
    picked = jnp.take(back_rows, target, axis=0).astype(jnp.float32)
    weighted = picked * route_weights.reshape(-1)[:, None]
    mixed = jnp.sum(weighted.reshape(tok_count, fanout, -1), axis=1)
    return mixed.astype(jnp.bfloat16)


LINK = 40e3
PAIR = 300e3


def edges(order, block, ring):
    place = dict(zip("zxy", block))
    stage = max([i for i, axis in enumerate(order) if place[axis]], default=-1)
    out = []
    for i in range(max(stage, 0), len(order)):
        axis = order[i]
        limit = ring - 1 if axis == "z" else 1
        if place[axis] < limit:
            out.append((axis, tuple(place[a] + (a == axis) for a in "zxy")))
    return out


def make_plan(parts, ring, rows, gate_us, down_us):
    heap, ops, count, free = [], [], itertools.count(), {}
    clock = 0.0

    def push(time, *event):
        heapq.heappush(heap, (time, next(count), event))

    def send(link, size, rate, delay):
        free[link] = max(clock, free.get(link, 0.0)) + size / rate
        return free[link] + delay

    held, finished, made, got = {}, {}, {}, {}
    blocks = [(z, x, y) for z in range(ring) for x in range(2) for y in range(2)]
    children = {(p, b): [c for _, c in edges(order, b, ring)] for p, (order, _, _) in enumerate(parts) for b in blocks}
    parent = {(p, c): b for (p, b), cs in children.items() for c in cs}

    def hold(block):
        key = (block[0], block[2])
        held[key] = held.get(key, 0) + 1
        if held[key] == 4 * len(parts):
            push(clock, "gate", *key)

    def reach(p, block):
        got[p, block] = got.get((p, block), 0) + 1
        if got[p, block] == 1 + len(children[p, block]):
            push(clock, "sum", p, block)

    for p in range(len(parts)):
        push(0.0, "have", p, (0, 0, 0))
    while heap:
        time, _, event = heapq.heappop(heap)
        clock = max(clock, time)
        ops.append(event)
        kind = event[0]
        if kind == "have":
            _, p, block = event
            order, _, width = parts[p]
            for axis, child in edges(order, block, ring):
                push(send(axis, rows * width * 2, LINK, 1.6), "have", p, child)
            push(send("core", rows * width * 2, PAIR, 0.9), "mate", p, block)
            hold(block)
        elif kind == "mate":
            hold(event[2])
        elif kind == "gate":
            clock += gate_us
            finished[event[1]] = finished.get(event[1], 0) + 1
            if finished[event[1]] == 2:
                for y in (1, 0):
                    push(clock, "down", event[1], y)
        elif kind == "down":
            clock += down_us
            width = sum(part[2] for part in parts)
            for x in (1, 0):
                push(send("core", rows * width * 2, PAIR, 0.9), "back", (event[1], x, event[2]))
        elif kind == "back":
            for p in range(len(parts)):
                reach(p, event[1])
        elif kind == "sum":
            _, p, block = event
            clock += 0.1
            if (p, block) in parent:
                axis = [a for a, i, j in zip("zxy", block, parent[p, block]) if i != j][0]
                push(send(axis, rows * parts[p][2] * 2, LINK, 1.6), "came", p, block)
        elif kind == "came":
            reach(event[1], parent[event[1], event[2]])
    return ops, children, parent


def layer_kernel(parts, ring, plan, tokens, shares, gate_hbm, up_hbm, down_hbm, out, everything, w_gate, w_up, w_down,
                 gate_acc, up_acc, hidden, result, mate_rows, landed, weights, own_sem, load_sem, have_send, have_recv,
                 mate_send, mate_recv, back_send, back_recv, sum_send, sum_recv, share_send, share_recv):
    ops, children, parent = plan
    ep, tp = lax.axis_index("ep"), lax.axis_index("tp")
    core, side, level = lax.rem(ep, 2), lax.rem(ep // 2, 2), ep // 4
    rows, half = tokens.shape
    group = 4 * rows

    def device(z=0, x=0, y=0, c=0):
        new_z = lax.rem(level + z + ring, ring)
        new_x = lax.rem(side + x, 2)
        return (new_z * 2 + new_x) * 2 + lax.rem(core + c, 2), lax.rem(tp + y, 2)

    def number(block):
        return (block[0] * 2 + block[1]) * 2 + block[2]

    def place(block, c=0):
        return pl.ds(((block[0] * 2 + block[1]) * 2 + c) * rows, rows)

    def pair_place(block):
        return pl.ds((block[0] * 2 + block[1]) * rows, rows)

    def columns(p):
        return pl.ds(parts[p][1], parts[p][2])

    def remote(src, dst, send, recv, target):
        return pltpu.make_async_remote_copy(src_ref=src, dst_ref=dst, send_sem=send, recv_sem=recv,
                                            device_id=target, device_id_type=pl.DeviceIdType.MESH)

    def have_copy(p, child, axis):
        block = tuple(v - (a == axis) for a, v in zip("zxy", child))
        if block == (0, 0, 0):
            src = tokens.at[:, columns(p)]
        else:
            src = everything.at[block[2], place(block), columns(p)]
        return remote(src, everything.at[child[2], place(child), columns(p)], have_send.at[p, number(child)],
                      have_recv.at[p, number(child)], device(**{axis: 1}))

    def mate_copy(p, block):
        if block == (0, 0, 0):
            src = tokens.at[:, columns(p)]
        else:
            src = everything.at[block[2], place(block), columns(p)]
        return remote(src, everything.at[block[2], place(block, 1), columns(p)], mate_send.at[p, number(block)],
                      mate_recv.at[p, number(block)], device(c=1))

    def back_copy(block):
        return remote(result.at[block[2], place(block, 1)], mate_rows.at[block[2], pair_place(block)],
                      back_send.at[number(block)], back_recv.at[number(block)], device(c=1))

    def sum_copy(p, block):
        axis = [a for a, i, j in zip("zxy", block, parent[p, block]) if i != j][0]
        return remote(result.at[block[2], place(block), columns(p)], landed.at[block[2], pair_place(block), columns(p)],
                      sum_send.at[p, number(block)], sum_recv.at[p, number(block)], device(**{axis: -1 if axis == "z" else 1}))

    peers = [(z, x, c) for z in range(ring) for x in range(2) for c in range(2) if (z, x, c) != (0, 0, 0)]

    def share_copy(peer):
        z, x, c = peer
        target = device(z=z, x=x, c=c)
        i = number(peer)
        return remote(shares.at[target[0]], weights.at[i], share_send.at[i], share_recv.at[i], target)

    loads = []
    for y in range(2):
        at = lax.rem(tp + y, 2) * half
        loads.append([
            pltpu.make_async_copy(gate_hbm.at[pl.ds(at, half)], w_gate.at[y], load_sem.at[y, 0]),
            pltpu.make_async_copy(up_hbm.at[pl.ds(at, half)], w_up.at[y], load_sem.at[y, 1]),
            pltpu.make_async_copy(down_hbm.at[:, pl.ds(pl.multiple_of(at, 128), half)], w_down.at[y], load_sem.at[y, 2]),
        ])
    own = pltpu.make_async_copy(tokens, everything.at[0, pl.ds(0, rows)], own_sem)
    own_share = pltpu.make_async_copy(shares.at[ep], weights.at[0], share_send.at[0])

    barrier = pltpu.get_barrier_semaphore()
    greeted = [device(z=z, x=x, c=c) for z, x, c in peers] + [device(y=1)]
    for target in greeted:
        pl.semaphore_signal(barrier, inc=1, device_id=target, device_id_type=pl.DeviceIdType.MESH)
    own.start()
    own_share.start()
    for kind in ((0, 1), (2,)):
        for y in range(2):
            for i in kind:
                loads[y][i].start()
    pl.semaphore_wait(barrier, len(greeted))
    for peer in peers:
        share_copy(peer).start()

    waited = set()

    def once(key, copy):
        if key not in waited:
            waited.add(key)
            copy.wait()

    def gate(z, y, first, last):
        once("own", own)
        once(("load", y, 0), loads[y][0])
        once(("load", y, 1), loads[y][1])
        here = pl.ds(z * group, group)
        tile = 512 if half % 512 == 0 else 128
        if first:
            gate_acc[here] = jnp.zeros((group, gate_acc.shape[1]), jnp.float32)
            up_acc[here] = jnp.zeros((group, gate_acc.shape[1]), jnp.float32)

        def step(k, carry):
            depth = pl.ds(pl.multiple_of(k * tile, tile), tile)
            x = everything[y, here, depth]
            gate_acc[here] += jnp.dot(x, w_gate[y, depth], preferred_element_type=jnp.float32)
            up_acc[here] += jnp.dot(x, w_up[y, depth], preferred_element_type=jnp.float32)
            return carry

        lax.fori_loop(0, half // tile, step, 0)
        if last:
            for x in range(2):
                for c in range(2):
                    i = number((z, x, c))
                    if i:
                        share_copy((z, x, c)).wait_recv()
                    else:
                        own_share.wait()
                    row = lax.broadcasted_iota(jnp.int32, (rows, 128), 0)
                    lane = lax.broadcasted_iota(jnp.int32, (rows, 128), 1)
                    spread = jnp.broadcast_to(weights[i, 0:1, :], (rows, 128))
                    weight = jnp.sum(jnp.where(row == lane, spread, 0.0), axis=1, keepdims=True)
                    at = pl.ds(i * rows, rows)
                    g = gate_acc[at]
                    hidden[at] = (g / (1.0 + jnp.exp(-g)) * up_acc[at] * weight).astype(hidden.dtype)

    def down(z, y):
        once(("load", y, 2), loads[y][2])
        here = pl.ds(z * group, group)
        tile = 512 if half % 512 == 0 else 128

        def step(k, carry):
            across = pl.ds(pl.multiple_of(k * tile, tile), tile)
            result[y, here, across] = jnp.dot(
                hidden[here], w_down[y, :, across], preferred_element_type=jnp.float32).astype(result.dtype)
            return carry

        lax.fori_loop(0, half // tile, step, 0)

    gates, sent = {}, []
    for event in ops:
        kind = event[0]
        if kind == "have":
            _, p, block = event
            if block != (0, 0, 0):
                axis = [a for a, i, j in zip("zxy", block, parent[p, block]) if i != j][0]
                have_copy(p, block, axis).wait_recv()
            for axis, child in edges(parts[p][0], block, ring):
                have_copy(p, child, axis).start()
                sent.append(have_copy(p, child, axis))
            mate_copy(p, block).start()
            sent.append(mate_copy(p, block))
        elif kind == "mate":
            mate_copy(event[1], event[2]).wait_recv()
        elif kind == "gate":
            z, y = event[1:]
            gates[z] = gates.get(z, 0) + 1
            gate(z, y, gates[z] == 1, gates[z] == 2)
        elif kind == "down":
            z, y = event[1:]
            down(z, y)
            for x in (1, 0):
                back_copy((z, x, y)).start()
                sent.append(back_copy((z, x, y)))
        elif kind == "back":
            back_copy(event[1]).wait_recv()
        elif kind == "came":
            sum_copy(event[1], event[2]).wait_recv()
        elif kind == "sum":
            _, p, block = event
            y = block[2]
            total = result[y, place(block), columns(p)].astype(jnp.float32)
            total += mate_rows[y, pair_place(block), columns(p)].astype(jnp.float32)
            for child in children[p, block]:
                total += landed[child[2], pair_place(child), columns(p)].astype(jnp.float32)
            if (p, block) in parent:
                result[y, place(block), columns(p)] = total.astype(result.dtype)
                sum_copy(p, block).start()
                sent.append(sum_copy(p, block))
            else:
                out[:, columns(p)] = total.astype(out.dtype)
    for copy in sent:
        copy.wait_send()
    for peer in peers:
        share_copy(peer).wait_send()


def by_tokens(tokens, routes, route_weights, gate_proj, up_proj, down_proj):
    experts = lax.axis_size("ep")
    rows, half = tokens.shape
    depth = gate_proj.shape[2]
    ring = experts // 4
    chosen = routes[:, :, None] == jnp.arange(experts, dtype=jnp.int32)
    dense = jnp.sum(jnp.where(chosen, route_weights[:, :, None], 0.0), axis=1)
    shares = jnp.pad(dense.T, ((0, 0), (0, 128 - rows)))
    shares = jnp.broadcast_to(shares[:, None, :], (experts, 8, 128))
    tiles = half // 128
    most = max(1, tiles * 11 // 28)
    widths = [tiles - 2 * most, most, most]
    parts, at = [], 0
    for order, width in zip(("xyz", "zxy", "zyx"), widths):
        parts.append((order, at * 128, width * 128))
        at += width
    plan = make_plan(parts, ring, rows, 2.4, 1.6)
    count, total = 4 * ring, experts * rows
    any_space = pl.BlockSpec(memory_space=pl.ANY)
    vmem = pl.BlockSpec(memory_space=pltpu.VMEM)
    dma = pltpu.SemaphoreType.DMA
    bf16, f32 = jnp.bfloat16, jnp.float32
    return pl.pallas_call(
        functools.partial(layer_kernel, parts, ring, plan),
        out_shape=jax.ShapeDtypeStruct(tokens.shape, tokens.dtype),
        in_specs=[vmem, vmem, any_space, any_space, any_space],
        out_specs=vmem,
        scratch_shapes=[
            pltpu.VMEM((2, total, half), bf16),
            pltpu.VMEM((2, half, depth), bf16),
            pltpu.VMEM((2, half, depth), bf16),
            pltpu.VMEM((2, depth, half), bf16),
            pltpu.VMEM((total, depth), f32),
            pltpu.VMEM((total, depth), f32),
            pltpu.VMEM((total, depth), bf16),
            pltpu.VMEM((2, total, half), bf16),
            pltpu.VMEM((2, total // 2, half), bf16),
            pltpu.VMEM((2, total // 2, half), bf16),
            pltpu.VMEM((experts, 8, 128), f32),
            dma, dma((2, 3)),
            dma((3, count)), dma((3, count)),
            dma((3, count)), dma((3, count)),
            dma((count,)), dma((count,)),
            dma((3, count)), dma((3, count)),
            dma((experts,)), dma((experts,)),
        ],
        compiler_params=pltpu.CompilerParams(
            collective_id=0, has_side_effects=True, vmem_limit_bytes=60 << 20),
    )(tokens, shares, gate_proj[0], up_proj[0], down_proj[0])


def per_device(tokens, routes, *rest):
    tok_count = tokens.shape[0]
    capacity = min(tok_count, max(2, 2 * tok_count * routes.shape[1] // lax.axis_size("ep")))
    if capacity == tok_count and tok_count % 16 == 0 and tok_count <= 128 and lax.axis_size("ep") % 4 == 0 and lax.axis_size("tp") == 2:
        return by_tokens(tokens, routes, *rest)
    return by_slots(tokens, routes, *rest, capacity)


def solution(mesh):
    in_specs = (
        P("ep", "tp"),
        P("ep", None),
        P("ep", None),
        P("ep", None, "tp"),
        P("ep", None, "tp"),
        P("ep", "tp", None),
    )
    out_specs = P("ep", "tp")
    return jax.shard_map(
        per_device, mesh=mesh, in_specs=in_specs, out_specs=out_specs, check_vma=False
    )
```
